32 devices in a mesh: groups: 2 (over y), branch: 4 (over z), head: 4 (over x, core).
Axes of the slice: x: 2, y: 2, z: 4, core: 2. Of those that a mesh axis runs over, the one named last changes fastest.
Arguments:
- queries: bfloat16 [1536, 5120], P(('groups', 'branch'), 'head'), parts along dimension 0, may hold values from -6 to 6
- key_states: bfloat16 [1536, 1024], P(('groups', 'branch'), 'head'), parts along dimension 0, may hold values from -6 to 6
- value_states: bfloat16 [1536, 1024], P(('groups', 'branch'), 'head'), parts along dimension 0, may hold values from -6 to 6
- cotangent: bfloat16 [1536, 5120], P(('groups', 'branch'), 'head'), parts along dimension 0, may hold values from -48 to 48
- key_weight: bfloat16 [5120, 1024], P(None, 'head'), may hold values from -0.078125 to 0.078125
- value_weight: bfloat16 [5120, 1024], P(None, 'head'), may hold values from -0.078125 to 0.078125
- leaf_length: int32 [8], P(('groups', 'branch')), parts along dimension 0, may hold values from 32 to 128, as said below
Outputs:
- d_query: bfloat16 [1536, 5120], P(('groups', 'branch'), 'head'), parts along dimension 0
- d_input: bfloat16 [1536, 5120], P(('groups', 'branch', 'head')), parts along dimension 0
The draws below stay inside these ranges and needn't reach their ends.
There are 2 independent parts, one for each index of `groups`. The reference program is written for one: setup_inputs(seed, part) draws one part's arguments, and reference() takes and returns one part's arrays. A program takes and returns all parts, laid end to end along the dimension named above; an argument that names none is the same for every part. Nothing has to cross between parts.
Inputs may be any that keep to these rules, and one draw needn't show every extreme that they name: `leaf_length`: some leaf has exactly 128 live tokens.
All inputs are finite; a program needn't handle non-finite values.
Results may differ from the reference program's by a relative error of at most 0.012.
The reference program's roundings to bfloat16 on the way count: a program that leaves them out, or rounds other values in their place, can miss the bound.
Values may be sent and summed in bfloat16 or wider, within the bound.
A program may use at most 64 MiB of HBM per device.

```python
import jax
import jax.numpy as jnp
from jax import lax

D = 5120
QH = 40
KVH = 8
HD = 128
LEAF = 128
ANC = 32
LEVELS = 2
LEAVES = 4
TOKENS = 768
N_HEAD = 4


def draw_queries(key, part):
    shape_full = (TOKENS, QH * HD)
    entries = jax.random.normal(jax.random.fold_in(key, 1), shape_full, jnp.float32)
    return jnp.clip(entries, -6.0, 6.0).astype(jnp.bfloat16)


def draw_key_states(key, part):
    shape_full = (TOKENS, KVH * HD)
    entries = jax.random.normal(jax.random.fold_in(key, 4), shape_full, jnp.float32)
    return jnp.clip(entries, -6.0, 6.0).astype(jnp.bfloat16)


def draw_leaf_length(key, part):
    lengths = jax.random.randint(jax.random.fold_in(key, 11), (LEAVES,), LEAF // 4, LEAF + 1)
    full_leaf = jax.random.randint(jax.random.fold_in(key, 12), (), 0, LEAVES)
    return jnp.where(jnp.arange(LEAVES) == full_leaf, LEAF, lengths).astype(jnp.int32)


def block_scale(stream_key, shape, shards, least, high):
    factor_of, own = 1.0, jax.random.fold_in(stream_key, 6)
    for dim, shards_of in shards:
        steps = jnp.exp(jax.random.uniform(jax.random.fold_in(own, dim), (shards_of,), jnp.float32, least / len(shards), high / len(shards)))
        factor_of = factor_of * jnp.repeat(steps, shape[dim] // shards_of).reshape([-1 if axis == dim else 1 for axis in range(len(shape))])
    return factor_of


def centred(key, dims, spread, limit, split=(), kind=jnp.bfloat16):
    values = jax.random.normal(key, dims, jnp.float32) * spread
    if len(split) > 0:
        values = block_scale(key, dims, split, -0.22, 0.18) * values
    return jnp.clip(values, min=-limit, max=limit).astype(kind)


def setup_inputs(seed: int = 0, part: int = 0) -> dict:
    arg_keys = jax.random.split(jax.random.key(seed), 8)
    own_keys = jax.random.split(jax.random.fold_in(arg_keys[7], part), 8)
    queries = draw_queries(jax.random.fold_in(jax.random.fold_in(arg_keys[7], part), 71), part)
    key_states = draw_key_states(jax.random.fold_in(jax.random.fold_in(arg_keys[7], part), 71), part)
    value_states = centred(own_keys[2], (TOKENS, KVH * HD), 1.0, 6.0, ((0, 4), (1, 4)))
    cotangent = centred(own_keys[3], (TOKENS, QH * HD), 8.0, 48.0, ((0, 4), (1, 4)))
    key_weight = centred(arg_keys[4], (D, KVH * HD), D ** -0.5, 0.078125, ((1, 4),))
    value_weight = centred(arg_keys[5], (D, KVH * HD), D ** -0.5, 0.078125, ((1, 4),))
    leaf_length = draw_leaf_length(jax.random.fold_in(jax.random.fold_in(arg_keys[7], part), 71), part)
    return {"queries": queries, "key_states": key_states, "value_states": value_states, "cotangent": cotangent, "key_weight": key_weight, "value_weight": value_weight, "leaf_length": leaf_length}


def pick_segments(source, branch_pos):
    pieces = []
    for level_no in range(LEVELS, 0, -1):
        span_rows = 2 ** level_no
        first_row = (branch_pos // span_rows) * span_rows
        level_rows = source[:, LEAF + (level_no - 1) * ANC:LEAF + level_no * ANC]
        picked = lax.dynamic_slice_in_dim(level_rows, first_row, span_rows, 0)
        pieces.append(picked.reshape((span_rows * ANC,) + source.shape[2:]))
    own_block = lax.dynamic_index_in_dim(source, branch_pos, 0, keepdims=False)
    pieces.append(own_block[:LEAF])
    return jnp.concatenate(pieces, axis=0)


def rounded(values):
    return lax.optimization_barrier(values.astype(jnp.bfloat16)).astype(jnp.float32)


def reference(queries, key_states, value_states, cotangent, key_weight, value_weight, leaf_length):
    rows_dev = LEAF + LEVELS * ANC
    group_size = QH // KVH
    score_scale = HD ** -0.5
    kv_width = KVH * HD
    query_all = queries.reshape(LEAVES, rows_dev, KVH, group_size, HD)
    key_all = key_states.reshape(LEAVES, rows_dev, KVH, HD)
    value_all = value_states.reshape(LEAVES, rows_dev, KVH, HD)
    d_all = cotangent.reshape(LEAVES, rows_dev, KVH, group_size, HD)

    def one_device(branch_pos):
        key_set = pick_segments(key_all, branch_pos).astype(jnp.float32)
        value_set = pick_segments(value_all, branch_pos).astype(jnp.float32)
        query_rows = lax.dynamic_index_in_dim(query_all, branch_pos, 0, keepdims=False).astype(jnp.float32)
        d_rows = lax.dynamic_index_in_dim(d_all, branch_pos, 0, keepdims=False).astype(jnp.float32)
        live_count = lax.dynamic_index_in_dim(leaf_length, branch_pos, 0, keepdims=False)
        key_level = jnp.concatenate([jnp.full((2 ** level_no * ANC,), level_no, jnp.int32) for level_no in range(LEVELS, 0, -1)] + [jnp.zeros((LEAF,), jnp.int32)])
        key_place = jnp.concatenate([jnp.arange(2 ** level_no * ANC, dtype=jnp.int32) for level_no in range(LEVELS, 0, -1)] + [jnp.arange(LEAF, dtype=jnp.int32)])
        query_level = jnp.concatenate([jnp.zeros((LEAF,), jnp.int32)] + [jnp.full((ANC,), level_no, jnp.int32) for level_no in range(1, LEVELS + 1)])
        query_place = jnp.concatenate([jnp.arange(LEAF, dtype=jnp.int32)] + [(branch_pos % (2 ** level_no)) * ANC + jnp.arange(ANC, dtype=jnp.int32) for level_no in range(1, LEVELS + 1)])
        allowed = (key_level[None, :] > query_level[:, None]) | ((key_level[None, :] == query_level[:, None]) & (key_place[None, :] <= query_place[:, None]))
        live_rows = (query_level > 0) | (query_place < live_count)
        d_rows = jnp.where(live_rows[:, None, None, None], d_rows, jnp.zeros_like(d_rows))
        scores = jnp.einsum("rgjd,kgd->gjrk", query_rows, key_set) * score_scale
        scores = jnp.where(allowed[None, None], scores, -jnp.inf)
        row_max = jnp.max(scores, axis=3, keepdims=True)
        exp_scores = jnp.exp(scores - row_max)
        attn_prob = exp_scores / jnp.sum(exp_scores, axis=3, keepdims=True)
        attn_low = rounded(attn_prob)
        attended = jnp.einsum("gjrk,kgd->rgjd", attn_low, value_set)
        row_delta = jnp.sum(d_rows * attended, axis=3)
        grad_prob = jnp.einsum("rgjd,kgd->gjrk", d_rows, value_set)
        grad_score = rounded(attn_prob * (grad_prob - jnp.transpose(row_delta, (1, 2, 0))[:, :, :, None]))
        grad_query = jnp.einsum("gjrk,kgd->rgjd", grad_score, key_set) * score_scale
        grad_key = jnp.einsum("gjrk,rgjd->kgd", grad_score, query_rows) * score_scale
        grad_value = jnp.einsum("gjrk,rgjd->kgd", attn_low, d_rows)
        return grad_query.reshape(rows_dev, QH * HD).astype(jnp.bfloat16), grad_key, grad_value

    grad_query, grad_key, grad_value = lax.map(one_device, jnp.arange(LEAVES, dtype=jnp.int32))

    def assemble(partial_all):
        key_total = partial_all.shape[1]
        level_parts = []
        offset = 0
        for level_no in range(LEVELS, 0, -1):
            span_rows = 2 ** level_no
            segment_rows = partial_all[:, offset:offset + span_rows * ANC].reshape(LEAVES // span_rows, span_rows, span_rows * ANC, KVH, HD)
            level_parts.append(jnp.sum(segment_rows, axis=1).reshape(LEAVES, ANC, KVH, HD))
            offset = offset + span_rows * ANC
        leaf_part = partial_all[:, key_total - LEAF:]
        whole = jnp.concatenate([leaf_part] + level_parts[::-1], axis=1)
        return whole.reshape(TOKENS, kv_width).astype(jnp.bfloat16)

    d_key = assemble(grad_key)
    d_value = assemble(grad_value)
    per_group = (KVH // N_HEAD) * HD
    input_sum = jnp.zeros((TOKENS, D), jnp.float32)
    for head_no in range(N_HEAD):
        low_col = head_no * per_group
        partial_sum = jnp.dot(d_key[:, low_col:low_col + per_group], key_weight[:, low_col:low_col + per_group].T, preferred_element_type=jnp.float32)
        partial_sum = partial_sum + jnp.dot(d_value[:, low_col:low_col + per_group], value_weight[:, low_col:low_col + per_group].T, preferred_element_type=jnp.float32)
        input_sum = input_sum + rounded(partial_sum)
    return grad_query.reshape(TOKENS, QH * HD), input_sum.astype(jnp.bfloat16)
```

```python
import functools
import math

import jax
import jax.numpy as jnp
from jax import lax
from jax.experimental import pallas as pl
from jax.experimental.pallas import tpu as pltpu
from jax.sharding import PartitionSpec as P

HD = 128
ANC = 32
NEG = -1e30
NT = (((1,), (1,)), ((), ()))
NN = (((1,), (0,)), ((), ()))
BF = jnp.bfloat16
F32 = jnp.float32


def dot(a, b, dims):
    return lax.dot_general(a, b, dims, preferred_element_type=F32)


def flipped(value, mask):
    out = value
    for bit in range(mask.bit_length()):
        if mask >> bit & 1:
            out = out + (1 - 2 * lax.rem(lax.div(value, 1 << bit), 2)) * (1 << bit)
    return out


class Plan:
    def __init__(self, branch, head, rows, kv_cols, q_cols, width):
        self.branch, self.head, self.rows = branch, head, rows
        self.levels = branch.bit_length() - 1
        self.leaf = rows - self.levels * ANC
        self.kv_cols, self.q_cols, self.width = kv_cols, q_cols, width
        self.kv = kv_cols // HD
        self.group = q_cols // kv_cols
        self.off = {}
        at = 0
        for level in range(self.levels, 0, -1):
            self.off[level] = at
            at += 2**level * ANC
        self.anc_keys = at
        self.keys = at + self.leaf
        self.anc_rows = self.levels * ANC
        self.together = self.group if self.keys <= 512 else 1
        self.lanes = -(-self.together * self.anc_rows // 128) * 128
        self.chunk = rows // head
        self.padded = -(-self.chunk // 16) * 16
        self.half = width // 2
        self.moves = [(l, d) for l in range(self.levels, 0, -1) for d in range(1, 2**l)]
        if self.padded == self.chunk:
            bounds = [(0, self.leaf), (self.leaf, rows)]
        else:
            bounds = [(0, head * self.padded)]
        self.phases = []
        count = 0
        for low, high in bounds:
            segs = []
            for j in range(head):
                a, b = max(low, j * self.padded), min(high, (j + 1) * self.padded)
                if a < b:
                    segs.append((count, j, a - j * self.padded, b - j * self.padded, a - low))
                    count += 1
            self.phases.append((low, high, segs))
        self.seg_count = count
        self.tiles = 2
        self.tile = self.half // self.tiles


def kernel(pn, len_ref, q_hbm, k_hbm, v_hbm, c_hbm, kw_hbm, vw_hbm, dq_hbm, di_hbm,
           qv, cv, kall, vall, kwv, vwv, dsl, pbl, dsa, pba, sendg, recvg, gr, gpad,
           psend, mrecv, psum, xrecv, dqv, outv,
           in_sem, own_sem, w_sem, ks_sem, kr_sem, gs_sem, gr_sem, ms_sem, mr_sem,
           xs_sem, xr_sem, out_sem):
    b = lax.axis_index("branch")
    me = lax.axis_index("head")
    core = lax.rem(me, 2)
    chip = lax.div(me, 2)
    mate = me + 1 - 2 * core
    leaf, anc, keys, group = pn.leaf, pn.anc_keys, pn.keys, pn.group
    scale = HD ** (-0.5)

    local = [
        pltpu.make_async_copy(q_hbm, qv, in_sem.at[0]),
        pltpu.make_async_copy(c_hbm, cv, in_sem.at[1]),
        pltpu.make_async_copy(k_hbm.at[pl.ds(0, leaf)], kall.at[pl.ds(anc, leaf)], in_sem.at[2]),
        pltpu.make_async_copy(v_hbm.at[pl.ds(0, leaf)], vall.at[pl.ds(anc, leaf)], in_sem.at[3]),
    ]
    for l in range(1, pn.levels + 1):
        src = pl.ds(leaf + (l - 1) * ANC, ANC)
        dst = pl.ds(pn.off[l], ANC)
        local.append(pltpu.make_async_copy(k_hbm.at[src], kall.at[dst], own_sem.at[0, l - 1]))
        local.append(pltpu.make_async_copy(v_hbm.at[src], vall.at[dst], own_sem.at[1, l - 1]))
    for copy in local:
        copy.start()
    weights = [
        pltpu.make_async_copy(kw_hbm, kwv, w_sem.at[0]),
        pltpu.make_async_copy(vw_hbm, vwv, w_sem.at[1]),
    ]

    barrier = pltpu.get_barrier_semaphore()
    for d in range(1, pn.branch):
        pl.semaphore_signal(barrier, inc=1, device_id={"branch": flipped(b, d)},
                            device_id_type=pl.DeviceIdType.MESH)
    for e in range(1, pn.head):
        pl.semaphore_signal(barrier, inc=1, device_id={"head": lax.rem(me + e, pn.head)},
                            device_id_type=pl.DeviceIdType.MESH)
    pl.semaphore_wait(barrier, pn.branch - 1 + pn.head - 1)

    gathers = []
    for no, (l, d) in enumerate(pn.moves):
        src = pl.ds(leaf + (l - 1) * ANC, ANC)
        dst = pl.ds(pn.off[l] + d * ANC, ANC)
        for which, (hbm, ref) in enumerate(((k_hbm, kall), (v_hbm, vall))):
            copy = pltpu.make_async_remote_copy(
                src_ref=hbm.at[src], dst_ref=ref.at[dst],
                send_sem=ks_sem.at[which, no], recv_sem=kr_sem.at[which, no],
                device_id={"branch": flipped(b, d)}, device_id_type=pl.DeviceIdType.MESH)
            copy.start()
            gathers.append(copy)
    for copy in weights:
        copy.start()

    live = lax.broadcasted_iota(jnp.int32, (leaf, HD), 0) < len_ref[0]
    causal = (lax.broadcasted_iota(jnp.int32, (leaf, leaf), 0)
              <= lax.broadcasted_iota(jnp.int32, (leaf, leaf), 1))
    lane = lax.broadcasted_iota(jnp.int32, (ANC, pn.lanes), 1)
    row = lax.broadcasted_iota(jnp.int32, (ANC, pn.lanes), 0)
    block = lax.shift_right_logical(lane, 5)
    wraps = jnp.zeros_like(block)
    for m in range(1, pn.together):
        wraps = wraps + jnp.where(block >= m * pn.levels, 1, 0)
    q_level = block - pn.levels * wraps + 1
    q_place = lane - 32 * block
    bias = []
    for l in range(pn.levels, 0, -1):
        for d in range(2**l):
            if d == 0:
                ok = (q_level < l) | ((q_level == l) & (row <= q_place))
            else:
                bit = lax.rem(lax.div(b, 1 << (d.bit_length() - 1)), 2)
                ok = q_level < l + bit
            bias.append(jnp.where(ok, 0.0, NEG).astype(F32))
    bias = jnp.concatenate(bias, axis=0)

    for copy in local:
        copy.wait()
    for copy in gathers:
        copy.wait_recv()

    def soft(scores, grad_prob):
        top = jnp.max(scores, axis=0, keepdims=True)
        e = jnp.exp2((scores - top) * (scale * math.log2(math.e)))
        p = e * (1.0 / jnp.sum(e, axis=0, keepdims=True))
        pb = p.astype(BF)
        delta = jnp.sum(pb.astype(F32) * grad_prob, axis=0, keepdims=True)
        return pb, (p * (grad_prob - delta)).astype(BF)

    sends = []
    for g in range(pn.kv):
        cols = slice(g * HD, (g + 1) * HD)
        kg, vg = kall[:, cols], vall[:, cols]
        kt = kg.astype(F32).T.astype(BF)
        ql, dl, qa, da = [], [], [], []
        for h in range(group):
            hc = slice((g * group + h) * HD, (g * group + h + 1) * HD)
            q = qv[0:leaf, hc]
            d = jnp.where(live, cv[0:leaf, hc].astype(F32), 0.0).astype(BF)
            ql.append(q)
            dl.append(d)
            qa.append(qv[leaf:, hc])
            da.append(cv[leaf:, hc])
            st = dot(kg, q, NT)
            gp = dot(vg, d, NT)
            st = jnp.concatenate([st[:anc], jnp.where(causal, st[anc:], NEG)], axis=0)
            pb, ds = soft(st, gp)
            pbl[:, h * leaf:(h + 1) * leaf] = pb
            dsl[:, h * leaf:(h + 1) * leaf] = ds
        pad = pn.lanes - pn.together * pn.anc_rows
        zeros = [jnp.zeros((pad, HD), BF)] if pad else []
        qs, dd = [], []
        for start in range(0, group, pn.together):
            qx = jnp.concatenate(qa[start:start + pn.together] + zeros, axis=0)
            dx = jnp.concatenate(da[start:start + pn.together] + zeros, axis=0)
            qs.append(qx)
            dd.append(dx)
            pb, ds = soft(dot(kg[:anc], qx, NT) + bias, dot(vg[:anc], dx, NT))
            at = start // pn.together * pn.lanes
            pba[:, at:at + pn.lanes] = pb
            dsa[:, at:at + pn.lanes] = ds
        ql = jnp.concatenate(ql, axis=0)
        dl = jnp.concatenate(dl, axis=0)
        qs = jnp.concatenate(qs, axis=0)
        dd = jnp.concatenate(dd, axis=0)
        gk = (dot(dsl[:anc], ql, NN) + dot(dsa[...], qs, NN)) * scale
        gv = dot(pbl[:anc], dl, NN) + dot(pba[...], dd, NN)
        sendg[g, :, 0:HD] = gk.astype(BF)
        sendg[g, :, HD:2 * HD] = gv.astype(BF)
        for no, (l, d) in enumerate(pn.moves):
            where = pl.ds(pn.off[l] + d * ANC, ANC)
            copy = pltpu.make_async_remote_copy(
                src_ref=sendg.at[g, where], dst_ref=recvg.at[g, where],
                send_sem=gs_sem.at[g, no], recv_sem=gr_sem.at[g, no],
                device_id={"branch": flipped(b, d)}, device_id_type=pl.DeviceIdType.MESH)
            copy.start()
            sends.append(copy)
        kc = slice(g * HD, (g + 1) * HD)
        vc = slice(pn.kv_cols + g * HD, pn.kv_cols + (g + 1) * HD)
        for l in range(1, pn.levels + 1):
            rows = slice(leaf + (l - 1) * ANC, leaf + l * ANC)
            gr[rows, kc] = gk[pn.off[l]:pn.off[l] + ANC]
            gr[rows, vc] = gv[pn.off[l]:pn.off[l] + ANC]
        gr[0:leaf, kc] = dot(dsl[anc:], ql, NN) * scale
        gr[0:leaf, vc] = dot(pbl[anc:], dl, NN)
        dq = dot(kt, dsl[...], NN)
        for h in range(group):
            hc = slice((g * group + h) * HD, (g * group + h + 1) * HD)
            dqv[0:leaf, hc] = (dq[:, h * leaf:(h + 1) * leaf].T * scale).astype(BF)
        dqa = (dot(kt[:, :anc], dsa[...], NN).T * scale).astype(BF)
        for h in range(group):
            hc = slice((g * group + h) * HD, (g * group + h + 1) * HD)
            at = h // pn.together * pn.lanes + h % pn.together * pn.anc_rows
            dqv[leaf:, hc] = dqa[at:at + pn.anc_rows]

    dq_out = pltpu.make_async_copy(dqv, dq_hbm, out_sem.at[0])
    dq_out.start()
    for copy in weights:
        copy.wait()

    mine0 = core * pn.half
    other0 = (1 - core) * pn.half

    def reduce_anc():
        for copy in sends:
            copy.wait_recv()
        for g in range(pn.kv):
            for l in range(1, pn.levels + 1):
                rows = slice(leaf + (l - 1) * ANC, leaf + l * ANC)
                total = recvg[g, pn.off[l] + ANC:pn.off[l] + 2 * ANC].astype(F32)
                for d in range(2, 2**l):
                    at = pn.off[l] + d * ANC
                    total = total + recvg[g, at:at + ANC].astype(F32)
                kc = slice(g * HD, (g + 1) * HD)
                vc = slice(pn.kv_cols + g * HD, pn.kv_cols + (g + 1) * HD)
                gr[rows, kc] = gr[rows, kc] + total[:, :HD]
                gr[rows, vc] = gr[rows, vc] + total[:, HD:]

    waits = []
    exchanges = []
    for phase, (low, high, segs) in enumerate(pn.phases):
        if phase == len(pn.phases) - 1:
            reduce_anc()
        if pn.padded == pn.chunk:
            grads = gr[low:high]
        else:
            gpad[...] = jnp.zeros_like(gpad)
            for j in range(pn.head):
                gpad[j * pn.padded:j * pn.padded + pn.chunk] = gr[j * pn.chunk:(j + 1) * pn.chunk]
            grads = gpad[...]
        grads = grads.astype(BF)
        gk, gv = grads[:, :pn.kv_cols], grads[:, pn.kv_cols:]

        def part(start):
            rows = pl.ds(pl.multiple_of(start, 128), pn.tile)
            return (dot(gk, kwv[rows, :], NT) + dot(gv, vwv[rows, :], NT)).astype(BF)

        mates = []
        for t in range(pn.tiles):
            where = (pl.ds(low, high - low), pl.ds(t * pn.tile, pn.tile))
            psend[low:high, t * pn.tile:(t + 1) * pn.tile] = part(other0 + t * pn.tile)
            copy = pltpu.make_async_remote_copy(
                src_ref=psend.at[where], dst_ref=mrecv.at[where],
                send_sem=ms_sem.at[phase, t], recv_sem=mr_sem.at[phase, t],
                device_id={"head": mate}, device_id_type=pl.DeviceIdType.MESH)
            copy.start()
            mates.append(copy)
            waits.append(copy)
        for t in range(pn.tiles):
            mine = part(mine0 + t * pn.tile).astype(F32)
            mates[t].wait_recv()
            tc = slice(t * pn.tile, (t + 1) * pn.tile)
            both = (mine + mrecv[low:high, tc].astype(F32)).astype(BF)
            for no, j, r0, r1, at in segs:
                psum[j, r0:r1, tc] = both[at:at + r1 - r0]
                where = (pl.ds(r0, r1 - r0), pl.ds(t * pn.tile, pn.tile))
                copy = pltpu.make_async_remote_copy(
                    src_ref=psum.at[(j,) + where], dst_ref=xrecv.at[(me,) + where],
                    send_sem=xs_sem.at[no, t], recv_sem=xr_sem.at[me, no, t],
                    device_id={"head": j}, device_id_type=pl.DeviceIdType.MESH)
                exchanges.append((j, copy))

                @pl.when(me != j)
                def _(copy=copy):
                    copy.start()

    for phase, (low, high, segs) in enumerate(pn.phases):
        for t in range(pn.tiles):
            for no, j, r0, r1, at in segs:
                @pl.when(me == j)
                def _(no=no, j=j, r0=r0, r1=r1, t=t):
                    where = (pl.ds(r0, r1 - r0), pl.ds(t * pn.tile, pn.tile))
                    for e in range(1, pn.head):
                        peer = lax.rem(me + e, pn.head)
                        pltpu.make_async_remote_copy(
                            src_ref=psum.at[(j,) + where], dst_ref=xrecv.at[(peer,) + where],
                            send_sem=xs_sem.at[no, t], recv_sem=xr_sem.at[peer, no, t],
                            device_id={"head": peer},
                            device_id_type=pl.DeviceIdType.MESH).wait_recv()

    chips = pn.head // 2
    own = psum[me].astype(F32)
    for e in range(1, chips):
        own = own + xrecv[2 * lax.rem(chip + e, chips) + core].astype(F32)
    outv[0] = own[:pn.chunk].astype(BF)
    rest = xrecv[mate].astype(F32)
    for e in range(1, chips):
        rest = rest + xrecv[2 * lax.rem(chip + e, chips) + 1 - core].astype(F32)
    outv[1] = rest[:pn.chunk].astype(BF)
    outs = [
        pltpu.make_async_copy(
            outv.at[i], di_hbm.at[:, pl.ds(pl.multiple_of(start, 128), pn.half)], out_sem.at[1 + i])
        for i, start in enumerate((mine0, other0))
    ]
    for copy in outs:
        copy.start()
    for copy in gathers + sends + waits:
        copy.wait_send()
    for j, copy in exchanges:
        @pl.when(me != j)
        def _(copy=copy):
            copy.wait_send()
    dq_out.wait()
    for copy in outs:
        copy.wait()


def solution(mesh):
    branch, head = mesh.shape["branch"], mesh.shape["head"]

    def local(queries, key_states, value_states, cotangent, key_weight, value_weight, leaf_length):
        rows, q_cols = queries.shape
        kv_cols, width = key_states.shape[1], key_weight.shape[0]
        pn = Plan(branch, head, rows, kv_cols, q_cols, width)
        hbm = pl.BlockSpec(memory_space=pl.ANY)
        vm = pltpu.VMEM
        dma = pltpu.SemaphoreType.DMA
        total = pn.head * pn.padded
        anc_cols = pn.group // pn.together * pn.lanes
        n = len(pn.moves)
        scratch = [
            vm((rows, q_cols), BF), vm((rows, q_cols), BF),
            vm((pn.keys, kv_cols), BF), vm((pn.keys, kv_cols), BF),
            vm((width, kv_cols), BF), vm((width, kv_cols), BF),
            vm((pn.keys, pn.group * pn.leaf), BF), vm((pn.keys, pn.group * pn.leaf), BF),
            vm((pn.anc_keys, anc_cols), BF), vm((pn.anc_keys, anc_cols), BF),
            vm((pn.kv, pn.anc_keys, 2 * HD), BF), vm((pn.kv, pn.anc_keys, 2 * HD), BF),
            vm((rows, 2 * kv_cols), F32),
            vm((total, 2 * kv_cols) if pn.padded != pn.chunk else (8, 128), F32),
            vm((total, pn.half), BF), vm((total, pn.half), BF),
            vm((head, pn.padded, pn.half), BF), vm((head, pn.padded, pn.half), BF),
            vm((rows, q_cols), BF), vm((2, pn.chunk, pn.half), BF),
            dma((4,)), dma((2, pn.levels)), dma((2,)),
            dma((2, n)), dma((2, n)), dma((pn.kv, n)), dma((pn.kv, n)),
            dma((len(pn.phases), pn.tiles)), dma((len(pn.phases), pn.tiles)),
            dma((pn.seg_count, pn.tiles)), dma((head, pn.seg_count, pn.tiles)),
            dma((3,)),
        ]
        return pl.pallas_call(
            functools.partial(kernel, pn),
            out_shape=(
                jax.ShapeDtypeStruct((rows, q_cols), BF),
                jax.ShapeDtypeStruct((pn.chunk, width), BF),
            ),
            in_specs=[pl.BlockSpec(memory_space=pltpu.SMEM)] + [hbm] * 6,
            out_specs=(hbm, hbm),
            scratch_shapes=scratch,
            compiler_params=pltpu.CompilerParams(
                collective_id=0, has_side_effects=True, vmem_limit_bytes=60 * 2**20
            ),
        )(leaf_length, queries, key_states, value_states, cotangent, key_weight, value_weight)

    placed = (
        P(("groups", "branch"), "head"),
        P(("groups", "branch"), "head"),
        P(("groups", "branch"), "head"),
        P(("groups", "branch"), "head"),
        P(None, "head"),
        P(None, "head"),
        P(("groups", "branch")),
    )
    return jax.shard_map(
        local,
        mesh=mesh,
        in_specs=placed,
        out_specs=(P(("groups", "branch"), "head"), P(("groups", "branch", "head"), None)),
        check_vma=False,
    )
```
